256 devices in a mesh: dp: 16 (over x, y), rows: 16 (over z, core).
Axes of the slice: x: 4, y: 4, z: 8, core: 2. Of those that a mesh axis runs over, the one named last changes fastest.
Arguments:
- scenes: bfloat16 [16, 256, 256, 384], P('dp', 'rows'), may hold values from -6 to 6
- prompt: bfloat16 [256, 256, 384], P('rows'), may hold values from -6 to 6
- cotangent: bfloat16 [16, 256, 256, 384], P('dp', 'rows'), may hold values from -6 to 6
- first_weight: bfloat16 [2, 8, 48, 48], replicated, may hold values from -0.625 to 0.625
- first_bias: float32 [2, 384], replicated, may hold values from -3 to 3
- second_weight: bfloat16 [2, 8, 48, 48], replicated, may hold values from -0.625 to 0.625
- second_bias: float32 [2, 384], replicated, may hold values from -3 to 3
Outputs:
- mixed: bfloat16 [16, 256, 256, 384], P('dp', 'rows')
- prompt_grad: float32 [256, 256, 384], P('rows', 'dp')
The draws below stay inside these ranges and needn't reach their ends.
All inputs are finite; a program needn't handle non-finite values.
Results may differ from the reference program's by a relative error of at most 0.014.
Values may be sent and summed in bfloat16 or wider, within the bound.
No kernel may reach another device: no remote copies, remote signals or barrier semaphores. Data moves between devices by JAX's collectives and lax.ppermute only.
A program may use at most 128 MiB of HBM per device.

```python
import math
import jax
import jax.numpy as jnp
from jax import lax

H = 256
W = 256
C = 384
NB = 8
BS = 48
KW = 128
SCENES = 16
N_DP = 16


def raised(drawn, key, source, target, shards_of, factor):
    def block_of(position):
        return (jnp.arange(drawn.shape[position]) // (drawn.shape[position] // shards_of)).reshape((-1,) + (1,) * (drawn.ndim - 1 - position))

    near = jax.random.permutation(key, shards_of)[block_of(target)]
    far = (block_of(target) + shards_of // 2) % shards_of
    return jnp.where((block_of(source) == near) | (block_of(source) == far), factor * drawn, drawn)


def block_levels(key, shape, cuts, smallest, top_value):
    level = 1.0
    for dim, shards_of in cuts:
        heights = jax.random.uniform(jax.random.fold_in(jax.random.fold_in(key, 6), dim), (shards_of,), jnp.float32, smallest / len(cuts), top_value / len(cuts))
        level = level * jnp.repeat(jnp.exp(heights), shape[dim] // shards_of).reshape((-1,) + (1,) * (len(shape) - 1 - dim))
    return level


def scatter_about(key, extent, width, reach, cuts=(), kind=jnp.bfloat16):
    loudness = block_levels(key, extent, cuts, -0.22, 0.18) if cuts else 1.0
    result = jax.random.normal(key, extent, jnp.float32) * width * loudness
    return jnp.minimum(jnp.maximum(result, -reach), reach).astype(kind)


def gaussian_with(rng, shape, width, bound, cuts, heavy, kind=jnp.bfloat16):
    drawn = width * jax.random.normal(rng, shape, jnp.float32)
    if cuts:
        drawn = drawn * block_levels(rng, shape, cuts, -0.22, 0.18)
    return jnp.clip(raised(drawn, jax.random.fold_in(rng, 3), *heavy), -bound, bound).astype(kind)


def setup_inputs(seed: int = 0) -> dict:
    keys = jax.random.split(jax.random.key(seed), 8)
    scenes = scatter_about(keys[0], (SCENES, H, W, C), 1.0, 6.0, ((0, 16), (1, 16)))
    prompt = scatter_about(keys[1], (H, W, C), 1.0, 6.0, ((0, 16),))
    cotangent = gaussian_with(keys[2], (SCENES, H, W, C), 1.0, 6.0, ((0, 16), (1, 16)), (0, 2, 16, 2.0))
    first_weight = scatter_about(keys[3], (2, NB, BS, BS), (2 * BS) ** -0.5, 0.625)
    first_bias = scatter_about(keys[4], (2, C), 0.5, 3.0, (), jnp.float32)
    second_weight = scatter_about(keys[5], (2, NB, BS, BS), (2 * BS) ** -0.5, 0.625)
    second_bias = scatter_about(keys[6], (2, C), 0.5, 3.0, (), jnp.float32)
    return dict(scenes=scenes, prompt=prompt, cotangent=cotangent, first_weight=first_weight, first_bias=first_bias, second_weight=second_weight, second_bias=second_bias)


def product(form, left, right):
    return jnp.einsum(form, left.astype(jnp.float32), right.astype(jnp.float32), precision=lax.Precision.HIGHEST)

def row_tables():
    grid_index = jnp.arange(W, dtype=jnp.int32)
    mode_index = jnp.arange(KW, dtype=jnp.int32)
    phases = mode_index[:, None] * grid_index[None, :] % W
    angles = phases.astype(jnp.float32) * (2.0 * math.pi / W)
    factor = 1.0 / math.sqrt(W)
    cosine = jnp.cos(angles) * factor
    sines = jnp.sin(angles) * factor
    forward = jnp.stack([cosine, -sines], axis=0).astype(jnp.bfloat16)
    doubled = jnp.where(mode_index == 0, 1.0, 2.0).astype(jnp.float32)[:, None]
    inverse = jnp.stack([doubled * cosine, -doubled * sines], axis=0).astype(jnp.bfloat16)
    return (forward, jnp.transpose(inverse, (2, 0, 1)))

def column_tables():
    grid_index = jnp.arange(H, dtype=jnp.int32)
    phases = grid_index[:, None] * grid_index[None, :] % H
    angles = phases.astype(jnp.float32) * (2.0 * math.pi / H)
    factor = 1.0 / math.sqrt(H)
    cosine = jnp.cos(angles) * factor
    sines = jnp.sin(angles) * factor
    upper = jnp.stack([cosine, sines], axis=1)
    lower = jnp.stack([-sines, cosine], axis=1)
    forward = jnp.stack([upper, lower], axis=0).astype(jnp.bfloat16)
    return (forward, jnp.transpose(forward, (2, 3, 0, 1)))

def complex_block(weights):
    real_part = weights[0]
    imag_part = weights[1]
    first_row = jnp.stack([real_part, imag_part], axis=2)
    second_row = jnp.stack([-imag_part, real_part], axis=2)
    return jnp.stack([first_row, second_row], axis=0)

def spectral_mix(spectrum, first_block, second_block, first_bias, second_bias):
    layout = spectrum.shape
    pieces = spectrum.reshape(layout[:4] + (NB, BS))
    first_pre = product('smqkbi,qbipj->smpkbj', pieces, first_block) + first_bias.reshape(2, 1, NB, BS)
    hidden = jax.nn.gelu(first_pre, approximate=False).astype(jnp.bfloat16)
    second = product('smqkbi,qbipj->smpkbj', hidden, second_block) + second_bias.reshape(2, 1, NB, BS)
    return (second.astype(jnp.bfloat16).reshape(layout), first_pre)

def spectral_back(back_out, first_pre, first_block, second_block):
    layout = back_out.shape
    pieces = back_out.reshape(layout[:4] + (NB, BS))
    back_hidden = product('smpkbj,qbipj->smqkbi', pieces, second_block)
    cumulative = 0.5 * (1.0 + lax.erf(first_pre * 0.7071067811865476))
    density = jnp.exp(-0.5 * first_pre * first_pre) * 0.3989422804014327
    back_pre = (back_hidden * (cumulative + first_pre * density)).astype(jnp.bfloat16)
    back_spectrum = product('smpkbj,qbipj->smqkbi', back_pre, first_block)
    return back_spectrum.astype(jnp.bfloat16).reshape(layout)

def scene_pass(scene, cotangent, prompt, row_fwd, row_inv, column_fwd, column_inv, first_block, second_block, first_bias, second_bias):
    summed = (scene.astype(jnp.float32) + prompt.astype(jnp.float32)[None]).astype(jnp.bfloat16)
    row_spec = product('pkn,shnc->shpkc', row_fwd, summed).astype(jnp.bfloat16)
    back_spec = product('npk,shnc->shpkc', row_inv, cotangent).astype(jnp.bfloat16)
    spectrum = product('pmqh,shqkc->smpkc', column_fwd, row_spec).astype(jnp.bfloat16)
    output_spec, first_pre = spectral_mix(spectrum, first_block, second_block, first_bias, second_bias)
    grid_spec = product('phqm,smqkc->shpkc', column_inv, output_spec).astype(jnp.bfloat16)
    back_out = product('qhpm,shqkc->smpkc', column_inv, back_spec).astype(jnp.bfloat16)
    back_spectrum = spectral_back(back_out, first_pre, first_block, second_block)
    back_rows = product('pmqh,smpkc->shqkc', column_fwd, back_spectrum).astype(jnp.bfloat16)
    mixed = (summed.astype(jnp.float32) + product('npk,shpkc->shnc', row_inv, grid_spec)).astype(jnp.bfloat16)
    grad_terms = cotangent.astype(jnp.float32) + product('pkn,shpkc->shnc', row_fwd, back_rows)
    return (mixed, grad_terms)

def reference(scenes, prompt, cotangent, first_weight, first_bias, second_weight, second_bias):
    row_fwd, row_inv = row_tables()
    column_fwd, column_inv = column_tables()
    first_block = complex_block(first_weight)
    second_block = complex_block(second_weight)
    group_size = SCENES // N_DP

    def one_scene(partial_value, packed):
        scene, scene_cot = packed
        mixed, grad_terms = scene_pass(scene[None], scene_cot[None], prompt, row_fwd, row_inv, column_fwd, column_inv, first_block, second_block, first_bias, second_bias)
        return (partial_value + grad_terms[0], mixed[0])

    def one_group(totals, packed):
        group_scenes, group_cot = packed
        partial_value, mixed = lax.scan(one_scene, jnp.zeros((H, W, C), jnp.float32), (group_scenes, group_cot))
        rounded = lax.optimization_barrier(partial_value.astype(jnp.bfloat16)).astype(jnp.float32)
        return (totals + rounded, mixed)
    grouped_scenes = scenes.reshape((N_DP, group_size, H, W, C))
    grouped_cot = cotangent.reshape((N_DP, group_size, H, W, C))
    start = jnp.zeros((H, W, C), jnp.float32)
    prompt_grad, mixed = lax.scan(one_group, start, (grouped_scenes, grouped_cot))
    return (mixed.reshape((SCENES, H, W, C)), prompt_grad)
```

```python
import math

import jax
import jax.numpy as jnp
import numpy as np
from jax import lax
from jax.experimental import pallas as pl
from jax.experimental.pallas import tpu as pltpu
from jax.sharding import PartitionSpec as P


H = 256
W = 256
C = 384
NB = 8
BS = 48
KW = 128
N = 16
K8 = 8
BF = jnp.bfloat16
F32 = jnp.float32


def tables():
    grid = np.arange(W)
    modes = np.arange(KW)
    angles = ((modes[:, None] * grid[None, :]) % W).astype(np.float32) * np.float32(2.0 * math.pi / W)
    cosine = np.cos(angles) / np.float32(16.0)
    sine = np.sin(angles) / np.float32(16.0)
    forward = np.stack([cosine, -sine])
    doubled = np.where(modes == 0, 1.0, 2.0).astype(np.float32)[:, None]
    inverse = np.stack([doubled * cosine, -doubled * sine])

    def by_owner(table):
        return table.reshape(2, N, K8, W).transpose(1, 0, 2, 3).reshape(W, W).astype(BF)

    row_fwd, row_inv = by_owner(forward), by_owner(inverse)
    angles = ((grid[:, None] * grid[None, :]) % H).astype(np.float32) * np.float32(2.0 * math.pi / H)
    c = np.cos(angles) / np.float32(16.0)
    s = np.sin(angles) / np.float32(16.0)
    return row_fwd, row_inv, np.stack([c, s]).astype(BF)


ROW_FWD, ROW_INV, COL = tables()
TILE = (np.arange(C)[None, :] % BS == np.arange(BS)[:, None]).astype(BF)
BLOCK_OF = (np.arange(C)[:, None] // BS == np.arange(NB)[None, :]).astype(BF)


def dot(a, b):
    return jnp.dot(a, b, preferred_element_type=F32)


def cost(flops, bytes_accessed):
    return pl.CostEstimate(flops=int(flops), bytes_accessed=int(bytes_accessed), transcendentals=0)


def full(shape):
    return pl.BlockSpec(shape, lambda i: (0,) * len(shape))


HB = 2


def rows_scene_kernel(table, scene, prompt, out):
    for i in range(HB):
        summed = (scene[i].astype(F32) + prompt[i].astype(F32)).astype(BF)
        out[:, i] = dot(table[...], summed).astype(BF).reshape(N, 16, C)


def rows_cot_kernel(table, cot, out, pieces):
    for i in range(HB):
        x = cot[i]
        out[:, i] = dot(table[...], x).astype(BF).reshape(N, 16, C)
        pieces[:, i] = x.reshape(N, 16, C)


GRID_SPEC = pl.BlockSpec((HB, W, C), lambda i: (i, 0, 0))
SPEC_SPEC = pl.BlockSpec((N, HB, 16, C), lambda i: (0, i, 0, 0))
SPEC_SHAPE = jax.ShapeDtypeStruct((N, N, 16, C), BF)
ROW_FLOPS = 2 * 256 * 256 * N * C
ARRAY_BYTES = 2 * N * W * C


def rows_scene(scene, prompt):
    return pl.pallas_call(
        rows_scene_kernel,
        grid=(N // HB,),
        in_specs=[full((W, W)), GRID_SPEC, GRID_SPEC],
        out_specs=SPEC_SPEC,
        out_shape=SPEC_SHAPE,
        cost_estimate=cost(ROW_FLOPS, 3 * ARRAY_BYTES),
        name="rows_scene",
    )(ROW_FWD, scene, prompt)


def rows_cot(cot):
    return pl.pallas_call(
        rows_cot_kernel,
        grid=(N // HB,),
        in_specs=[full((W, W)), GRID_SPEC],
        out_specs=[SPEC_SPEC, SPEC_SPEC],
        out_shape=[SPEC_SHAPE, SPEC_SHAPE],
        cost_estimate=cost(ROW_FLOPS, 3 * ARRAY_BYTES),
        name="rows_cot",
    )(ROW_INV, cot)


LANES = 128
TILES = C // LANES


def load_block(received, wide):
    def step(r, carry):
        rows = received[r].astype(F32).reshape(256, C)
        for t in range(TILES):
            wide[t, pl.ds(pl.multiple_of(r * 256, 256), 256), :] = rows[:, t * LANES : (t + 1) * LANES]
        return carry

    lax.fori_loop(0, N, step, 0)


def block_of(wide, r):
    rows = pl.ds(pl.multiple_of(r * 256, 256), 256)
    return jnp.concatenate([wide[t, rows, :].astype(BF) for t in range(TILES)], axis=1).reshape(N, 16, C)


def columns_of(wide, k):
    halves = []
    for q in range(2):
        rows = pl.ds(q * K8 + k, H, stride=16)
        halves.append(jnp.concatenate([wide[t, rows, :].astype(BF) for t in range(TILES)], axis=1))
    return jnp.concatenate(halves, axis=0)


def store_columns(wide, k, value):
    for q in range(2):
        rows = pl.ds(q * K8 + k, H, stride=16)
        for t in range(TILES):
            wide[t, rows, :] = value[q * H : (q + 1) * H, t * LANES : (t + 1) * LANES]


def to_lanes(rows):
    return jnp.concatenate([rows[:H], rows[H:]], axis=1)


def to_rows(lanes):
    return jnp.concatenate([lanes[:, :C], lanes[:, C:]], axis=0)


def same_block(member):
    return lax.dot_general(member[...], member[...], (((1,), (1,)), ((), ())), preferred_element_type=F32)


def expand(weight, tile, member, dense):
    mask = same_block(member)
    real = (dot(weight[0], tile[...]) * mask).astype(BF)
    imag = (dot(weight[1], tile[...]) * mask).astype(BF)
    dense[:C, :C] = real
    dense[:C, C:] = imag
    dense[C:, :C] = -imag
    dense[C:, C:] = real


def expand_transposed(weight, tile, member, dense):
    mask = same_block(member)

    def spread(part):
        wide = lax.dot_general(tile[...], part, (((0,), (1,)), ((), ())), preferred_element_type=F32)
        return (wide * mask).astype(BF)

    real = spread(weight[0])
    imag = spread(weight[1])
    dense[:C, :C] = real
    dense[:C, C:] = -imag
    dense[C:, :C] = imag
    dense[C:, C:] = real


def mix_kernel(received, col, w1, b1, w2, b2, tile, member, out, slope, wide, dense1, dense2, col_fwd, col_inv):
    k = pl.program_id(0)

    @pl.when(k == 0)
    def _():
        load_block(received, wide)
        column_matrices(col, col_fwd, col_inv)
        expand(w1, tile, member, dense1)
        expand(w2, tile, member, dense2)

    spectrum = dot(col_fwd[...], columns_of(wide, k)).astype(BF)
    bias1 = jnp.concatenate([b1[0:1], b1[1:2]], axis=1)
    bias2 = jnp.concatenate([b2[0:1], b2[1:2]], axis=1)
    z = dot(to_lanes(spectrum), dense1[...]) + bias1
    cumulative = 0.5 * (1.0 + lax.erf(z * 0.7071067811865476))
    hidden = (z * cumulative).astype(BF)
    slope[0] = cumulative + z * (jnp.exp(-0.5 * z * z) * 0.3989422804014327)
    output = (dot(hidden, dense2[...]) + bias2).astype(BF)
    store_columns(wide, k, dot(col_inv[...], to_rows(output)))

    @pl.when(k == K8 - 1)
    def _():
        def step(r, carry):
            out[r] = block_of(wide, r)
            return carry

        lax.fori_loop(0, N, step, 0)


def back_kernel(received, slope, col, w1, w2, tile, member, out, wide, dense1, dense2, col_fwd, col_inv):
    k = pl.program_id(0)

    @pl.when(k == 0)
    def _():
        load_block(received, wide)
        column_matrices(col, col_fwd, col_inv)
        expand_transposed(w1, tile, member, dense1)
        expand_transposed(w2, tile, member, dense2)

    back_out = dot(col_fwd[...], columns_of(wide, k)).astype(BF)
    back_pre = (dot(to_lanes(back_out), dense2[...]) * slope[0]).astype(BF)
    back_spectrum = dot(back_pre, dense1[...]).astype(BF)
    store_columns(wide, k, dot(col_inv[...], to_rows(back_spectrum)))

    @pl.when(k == K8 - 1)
    def _():
        def step(r, carry):
            out[:, r] = block_of(wide, r)
            return carry

        lax.fori_loop(0, N, step, 0)


def column_matrices(col, col_fwd, col_inv):
    c, s = col[0], col[1]
    for matrix, sine in ((col_fwd, s), (col_inv, -s)):
        matrix[:H, :H] = c
        matrix[:H, H:] = sine
        matrix[H:, :H] = -sine
        matrix[H:, H:] = c


MIX_FLOPS = 2 * K8 * (2 * 512 * 512 * C + 2 * 256 * 768 * 768)
MIX_SCRATCH = [
    pltpu.VMEM((TILES, H * 16, LANES), F32),
    pltpu.VMEM((2 * C, 2 * C), BF),
    pltpu.VMEM((2 * C, 2 * C), BF),
    pltpu.VMEM((2 * H, 2 * H), BF),
    pltpu.VMEM((2 * H, 2 * H), BF),
]
SLOPE_SPEC = pl.BlockSpec((1, H, 2 * C), lambda i: (i, 0, 0))
SLOPE_SHAPE = jax.ShapeDtypeStruct((K8, H, 2 * C), F32)
FULL_SPEC = full((N, N, 16, C))


def mix(received, w1, b1, w2, b2):
    return pl.pallas_call(
        mix_kernel,
        grid=(K8,),
        in_specs=[
            FULL_SPEC,
            full((2, H, H)),
            full((2, C, BS)),
            full((2, C)),
            full((2, C, BS)),
            full((2, C)),
            full((BS, C)),
            full((C, NB)),
        ],
        out_specs=[FULL_SPEC, SLOPE_SPEC],
        out_shape=[SPEC_SHAPE, SLOPE_SHAPE],
        scratch_shapes=MIX_SCRATCH,
        cost_estimate=cost(MIX_FLOPS, 4 * ARRAY_BYTES),
        name="mix",
    )(received, COL, w1, b1, w2, b2, TILE, BLOCK_OF)


def back(received, slope, w1, w2):
    return pl.pallas_call(
        back_kernel,
        grid=(K8,),
        in_specs=[
            FULL_SPEC,
            SLOPE_SPEC,
            full((2, H, H)),
            full((2, C, BS)),
            full((2, C, BS)),
            full((BS, C)),
            full((C, NB)),
        ],
        out_specs=FULL_SPEC,
        out_shape=SPEC_SHAPE,
        scratch_shapes=MIX_SCRATCH,
        cost_estimate=cost(MIX_FLOPS, 4 * ARRAY_BYTES),
        name="back",
    )(received, slope, COL, w1, w2, TILE, BLOCK_OF)


def finish_kernel(table, spec, scene, prompt, out):
    for i in range(HB):
        summed = (scene[i].astype(F32) + prompt[i].astype(F32)).astype(BF).astype(F32)
        out[i] = (summed + dot(table[...], spec[:, i].reshape(W, C))).astype(BF)


def finish(spec, scene, prompt):
    return pl.pallas_call(
        finish_kernel,
        grid=(N // HB,),
        in_specs=[full((W, W)), SPEC_SPEC, GRID_SPEC, GRID_SPEC],
        out_specs=GRID_SPEC,
        out_shape=jax.ShapeDtypeStruct((N, W, C), BF),
        cost_estimate=cost(ROW_FLOPS, 4 * ARRAY_BYTES),
        name="finish",
    )(np.ascontiguousarray(ROW_INV.T), spec, scene, prompt)


def grad_row_kernel(table, spec, out):
    out[...] = dot(table[...], spec[...].reshape(W, C)).astype(BF).reshape(N, 16, C)


def grad_row(spec):
    return pl.pallas_call(
        grad_row_kernel,
        grid=(1,),
        in_specs=[full((W, W)), full((N, 16, C))],
        out_specs=full((N, 16, C)),
        out_shape=jax.ShapeDtypeStruct((N, 16, C), BF),
        cost_estimate=cost(ROW_FLOPS // N, 2 * ARRAY_BYTES // N),
        name="grad_row",
    )(np.ascontiguousarray(ROW_FWD.T), spec)


def shifted_sum(parts, axis, mine, perm_of):
    def piece_for(index):
        starts = [jnp.uint32(0)] * parts.ndim
        starts[axis] = index
        sizes = list(parts.shape)
        sizes[axis] = 1
        return lax.squeeze(lax.dynamic_slice(parts, starts, sizes), (axis,))

    total = piece_for(mine).astype(F32)
    for j in (1, 3, 2):
        piece = piece_for((mine + j) & 3)
        total = total + lax.ppermute(piece, "dp", perm_of(j)).astype(F32)
    return total


def along_x(j):
    return [(x * 4 + y, ((x + j) % 4) * 4 + y) for x in range(4) for y in range(4)]


def along_y(j):
    return [(x * 4 + y, x * 4 + (y + j) % 4) for x in range(4) for y in range(4)]


def sum_over_dp(pieces):
    me = lax.axis_index("dp").astype(jnp.uint32)
    x, y = me >> 2, me & 3
    split = pieces.reshape(4, 4, 2, N // 2, 16, C)
    first = shifted_sum(split[:, :, 0], 1, y, along_y).astype(BF)
    second = shifted_sum(split[:, :, 1], 0, x, along_x).astype(BF)
    first = shifted_sum(first, 0, x, along_x)
    second = shifted_sum(second, 0, y, along_y)
    return jnp.concatenate([first, second], axis=0)


def exchange(blocks, axis):
    return lax.all_to_all(blocks, axis, split_axis=0, concat_axis=0, tiled=True)


def on_device(scenes, prompt, cotangent, first_weight, first_bias, second_weight, second_bias):
    scene, cot = scenes[0], cotangent[0]
    w1 = first_weight.reshape(2, C, BS)
    w2 = second_weight.reshape(2, C, BS)
    scene_cols = exchange(rows_scene(scene, prompt), "rows")
    cot_rows, cot_pieces = rows_cot(cot)
    cot_cols = exchange(cot_rows, "rows")
    cot_sum = sum_over_dp(cot_pieces)
    scene_cols, cot_sum = lax.optimization_barrier((scene_cols, cot_sum))
    mixed_cols, slope = mix(scene_cols, w1, first_bias, w2, second_bias)
    mixed_rows = exchange(mixed_cols, "rows")
    grad_sum = sum_over_dp(back(cot_cols, slope, w1, w2)).astype(BF)
    mixed = finish(mixed_rows, scene, prompt)
    grad_rows = exchange(grad_row(exchange(grad_sum, "rows")), "dp")
    prompt_grad = grad_rows.astype(F32) + cot_sum
    return (mixed[None], prompt_grad)


def solution(mesh):
    return jax.shard_map(
        on_device,
        mesh=mesh,
        in_specs=(
            P("dp", "rows", None, None),
            P("rows", None, None),
            P("dp", "rows", None, None),
            P(),
            P(),
            P(),
            P(),
        ),
        out_specs=(P("dp", "rows", None, None), P("rows", "dp", None)),
        check_vma=False,
    )
```

```python
import math

import jax
import jax.numpy as jnp
import numpy as np
from jax import lax
from jax.experimental import pallas as pl
from jax.experimental.pallas import tpu as pltpu
from jax.sharding import PartitionSpec as P


H = 256
W = 256
C = 384
NB = 8
BS = 48
KW = 128
N = 16
K8 = 8
BF = jnp.bfloat16
F32 = jnp.float32


def tables():
    grid = np.arange(W)
    modes = np.arange(KW)
    angles = ((modes[:, None] * grid[None, :]) % W).astype(np.float32) * np.float32(2.0 * math.pi / W)
    cosine = np.cos(angles) / np.float32(16.0)
    sine = np.sin(angles) / np.float32(16.0)
    forward = np.stack([cosine, -sine])
    doubled = np.where(modes == 0, 1.0, 2.0).astype(np.float32)[:, None]
    inverse = np.stack([doubled * cosine, -doubled * sine])

    def by_owner(table):
        return table.reshape(2, N, K8, W).transpose(1, 0, 2, 3).reshape(W, W).astype(BF)

    row_fwd, row_inv = by_owner(forward), by_owner(inverse)
    angles = ((grid[:, None] * grid[None, :]) % H).astype(np.float32) * np.float32(2.0 * math.pi / H)
    c = np.cos(angles) / np.float32(16.0)
    s = np.sin(angles) / np.float32(16.0)
    return row_fwd, row_inv, np.stack([c, s]).astype(BF)


ROW_FWD, ROW_INV, COL = tables()
TILE = (np.arange(C)[None, :] % BS == np.arange(BS)[:, None]).astype(BF)
BLOCK_OF = (np.arange(C)[:, None] // BS == np.arange(NB)[None, :]).astype(BF)


def dot(a, b):
    return jnp.dot(a, b, preferred_element_type=F32)


def cost(flops, bytes_accessed):
    return pl.CostEstimate(flops=int(flops), bytes_accessed=int(bytes_accessed), transcendentals=0)


def full(shape):
    return pl.BlockSpec(shape, lambda i: (0,) * len(shape))


HB = 4
FINISH_A = 2
PAIRS = [(i, i + 1) for i in range(0, HB, 2)]


def beside(left, right):
    return jnp.concatenate([left, right], axis=1)


def summed_row(scene, prompt, i):
    return (scene[i].astype(F32) + prompt[i].astype(F32)).astype(BF)


def put_rows(out, pair, value):
    value = value.astype(BF)
    for i, part in zip(pair, (value[:, :C], value[:, C:])):
        out[:, i] = part.reshape(N, 16, C)


def rows_scene_kernel(table, scene, prompt, out):
    for i, j in PAIRS:
        summed = beside(summed_row(scene, prompt, i), summed_row(scene, prompt, j))
        put_rows(out, (i, j), dot(table[...], summed))


def rows_cot_kernel(me, here, table, cot, *rest):
    outs, pieces, ordered = rest[:N], rest[N : N + 4], rest[N + 4]

    @pl.when(pl.program_id(0) == 0)
    def _():
        for j in range(N):
            owner = (here[0] + j) & (N - 1)
            ordered[j * 16 : (j + 1) * 16] = table[pl.ds(pl.multiple_of(owner * 16, 16), 16), :]

    for i, j in PAIRS:
        value = dot(ordered[...], beside(cot[i], cot[j])).astype(BF)
        for step in range(N):
            part = value[step * 16 : (step + 1) * 16]
            outs[step][i] = part[:, :C]
            outs[step][j] = part[:, C:]

    x, y = me[0] >> 2, me[0] & 3

    def slot(b, carry):
        for a in range(4):
            owner = ((x + b) & 3) * 4 + ((y + a) & 3)
            rows = pl.ds(pl.multiple_of(owner * 16, 16), 16)
            for i in range(HB):
                pieces[a][b, i] = cot[i, rows, :]
        return carry

    lax.fori_loop(0, 4, slot, 0)


GRID_SPEC = pl.BlockSpec((HB, W, C), lambda i: (i, 0, 0))
SPEC_SPEC = pl.BlockSpec((N, HB, 16, C), lambda i: (0, i, 0, 0))
SPEC_SHAPE = jax.ShapeDtypeStruct((N, N, 16, C), BF)
PIECE_SHAPE = jax.ShapeDtypeStruct((4, N // 2, 16, C), BF)
ROW_FLOPS = 2 * 256 * 256 * N * C
ARRAY_BYTES = 2 * N * W * C
ME_SPEC = pl.BlockSpec(memory_space=pltpu.SMEM)


def rows_scene(scene, prompt):
    return pl.pallas_call(
        rows_scene_kernel,
        grid=(N // HB,),
        in_specs=[full((W, W)), GRID_SPEC, GRID_SPEC],
        out_specs=SPEC_SPEC,
        out_shape=SPEC_SHAPE,
        cost_estimate=cost(ROW_FLOPS, 3 * ARRAY_BYTES),
        name="rows_scene",
    )(ROW_FWD, scene, prompt)


def rows_cot(me, here, cot):
    return pl.pallas_call(
        rows_cot_kernel,
        grid=(N // HB,),
        in_specs=[ME_SPEC, ME_SPEC, full((W, W)), GRID_SPEC],
        out_specs=[pl.BlockSpec((HB, 16, C), lambda i: (i, 0, 0))] * N
        + [pl.BlockSpec((4, HB, 16, C), lambda i: (0, i, 0, 0))] * 4,
        out_shape=[jax.ShapeDtypeStruct((N, 16, C), BF)] * N + [jax.ShapeDtypeStruct((4, N, 16, C), BF)] * 4,
        scratch_shapes=[pltpu.VMEM((W, W), BF)],
        cost_estimate=cost(ROW_FLOPS, 3 * ARRAY_BYTES),
        name="rows_cot",
    )(me, here, ROW_INV, cot)


LANES = 128
TILES = C // LANES


def load_block(received, wide):
    def step(r, carry):
        rows = received[r].astype(F32).reshape(256, C)
        for t in range(TILES):
            wide[t, pl.ds(pl.multiple_of(r * 256, 256), 256), :] = rows[:, t * LANES : (t + 1) * LANES]
        return carry

    lax.fori_loop(0, N, step, 0)


def block_of(wide, r):
    rows = pl.ds(pl.multiple_of(r * 256, 256), 256)
    return jnp.concatenate([wide[t, rows, :].astype(BF) for t in range(TILES)], axis=1).reshape(N, 16, C)


def columns_of(wide, k):
    halves = []
    for q in range(2):
        parts = []
        for kk in range(2):
            rows = pl.ds(q * K8 + k + kk, H, stride=16)
            parts += [wide[t, rows, :].astype(BF) for t in range(TILES)]
        halves.append(jnp.concatenate(parts, axis=1))
    return jnp.concatenate(halves, axis=0)


def store_columns(wide, k, value):
    for q in range(2):
        for kk in range(2):
            rows = pl.ds(q * K8 + k + kk, H, stride=16)
            for t in range(TILES):
                lane = kk * C + t * LANES
                wide[t, rows, :] = value[q * H : (q + 1) * H, lane : lane + LANES]


def swap_pairs(value):
    return jnp.concatenate([beside(value[:H, :C], value[H:, :C]), beside(value[:H, C:], value[H:, C:])], axis=0)


def same_block(member):
    return lax.dot_general(member[...], member[...], (((1,), (1,)), ((), ())), preferred_element_type=F32)


def expand(weight, tile, member, dense):
    mask = same_block(member)
    real = (dot(weight[0], tile[...]) * mask).astype(BF)
    imag = (dot(weight[1], tile[...]) * mask).astype(BF)
    dense[:C, :C] = real
    dense[:C, C:] = imag
    dense[C:, :C] = -imag
    dense[C:, C:] = real


def expand_transposed(weight, tile, member, dense):
    mask = same_block(member)

    def spread(part):
        wide = lax.dot_general(tile[...], part, (((0,), (1,)), ((), ())), preferred_element_type=F32)
        return (wide * mask).astype(BF)

    real = spread(weight[0])
    imag = spread(weight[1])
    dense[:C, :C] = real
    dense[:C, C:] = -imag
    dense[C:, :C] = imag
    dense[C:, C:] = real


def mix_kernel(received, col, w1, b1, w2, b2, tile, member, out, slope, wide, dense1, dense2, col_fwd, col_inv):
    k = pl.program_id(0) * 2

    @pl.when(k == 0)
    def _():
        load_block(received, wide)
        column_matrices(col, col_fwd, col_inv)
        expand(w1, tile, member, dense1)
        expand(w2, tile, member, dense2)

    spectrum = dot(col_fwd[...], columns_of(wide, k)).astype(BF)
    bias1 = jnp.concatenate([b1[0:1], b1[1:2]], axis=1)
    bias2 = jnp.concatenate([b2[0:1], b2[1:2]], axis=1)
    z = dot(swap_pairs(spectrum), dense1[...]) + bias1
    cumulative = 0.5 * (1.0 + lax.erf(z * 0.7071067811865476))
    hidden = (z * cumulative).astype(BF)
    slope[...] = (cumulative + z * (jnp.exp(-0.5 * z * z) * 0.3989422804014327)).reshape(2, H, 2 * C)
    output = (dot(hidden, dense2[...]) + bias2).astype(BF)
    store_columns(wide, k, dot(col_inv[...], swap_pairs(output)))

    @pl.when(k == K8 - 2)
    def _():
        def step(r, carry):
            out[r] = block_of(wide, r)
            return carry

        lax.fori_loop(0, N, step, 0)


def back_kernel(me, here, *refs):
    received, (slope, col, w1, w2, tile, member), rest = refs[:N], refs[N : N + 6], refs[N + 6 :]
    pieces, (wide, dense1, dense2, col_fwd, col_inv, landed, arrived) = rest[:8], rest[8:]
    k = pl.program_id(0) * 2

    @pl.when(k == 0)
    def _():
        for j in range(N):
            pltpu.make_async_copy(received[j], landed.at[j], arrived.at[j]).start()
        column_matrices(col, col_fwd, col_inv)
        expand_transposed(w1, tile, member, dense1)
        expand_transposed(w2, tile, member, dense2)
        for j in range(N):
            pltpu.make_async_copy(received[j], landed.at[j], arrived.at[j]).wait()

        def step(j, carry):
            source = (here[0] - j) & (N - 1)
            rows = landed[j].astype(F32).reshape(256, C)
            for t in range(TILES):
                wide[t, pl.ds(pl.multiple_of(source * 256, 256), 256), :] = rows[:, t * LANES : (t + 1) * LANES]
            return carry

        lax.fori_loop(0, N, step, 0)

    back_out = dot(col_fwd[...], columns_of(wide, k)).astype(BF)
    back_pre = (dot(swap_pairs(back_out), dense2[...]) * slope[...].reshape(2 * H, 2 * C)).astype(BF)
    back_spectrum = dot(back_pre, dense1[...]).astype(BF)
    store_columns(wide, k, dot(col_inv[...], swap_pairs(back_spectrum)))

    @pl.when(k == K8 - 2)
    def _():
        x, y = me[0] >> 2, me[0] & 3
        for half in range(2):
            for a in range(4):
                for b in range(4):
                    jx, jy = (b, a) if half == 0 else (a, b)
                    owner = ((x + jx) & 3) * 4 + ((y + jy) & 3)

                    def step(r, carry, a=a, b=b, half=half, owner=owner):
                        rows = pl.ds(pl.multiple_of(((half * 8 + r) * 16 + owner) * 16, 16), 16)
                        block = jnp.concatenate([wide[t, rows, :].astype(BF) for t in range(TILES)], axis=1)
                        pieces[half * 4 + a][b, r] = block
                        return carry

                    lax.fori_loop(0, N // 2, step, 0)


def column_matrices(col, col_fwd, col_inv):
    c, s = col[0], col[1]
    for matrix, sine in ((col_fwd, s), (col_inv, -s)):
        matrix[:H, :H] = c
        matrix[:H, H:] = sine
        matrix[H:, :H] = -sine
        matrix[H:, H:] = c


MIX_FLOPS = 2 * K8 * (2 * 512 * 512 * C + 2 * 256 * 768 * 768)
MIX_SCRATCH = [
    pltpu.VMEM((TILES, H * 16, LANES), F32),
    pltpu.VMEM((2 * C, 2 * C), BF),
    pltpu.VMEM((2 * C, 2 * C), BF),
    pltpu.VMEM((2 * H, 2 * H), BF),
    pltpu.VMEM((2 * H, 2 * H), BF),
]
SLOPE_SPEC = pl.BlockSpec((2, H, 2 * C), lambda i: (i, 0, 0))
SLOPE_SHAPE = jax.ShapeDtypeStruct((K8, H, 2 * C), F32)
FULL_SPEC = full((N, N, 16, C))


def mix(received, w1, b1, w2, b2):
    return pl.pallas_call(
        mix_kernel,
        grid=(K8 // 2,),
        in_specs=[
            FULL_SPEC,
            full((2, H, H)),
            full((2, C, BS)),
            full((2, C)),
            full((2, C, BS)),
            full((2, C)),
            full((BS, C)),
            full((C, NB)),
        ],
        out_specs=[FULL_SPEC, SLOPE_SPEC],
        out_shape=[SPEC_SHAPE, SLOPE_SHAPE],
        scratch_shapes=MIX_SCRATCH,
        cost_estimate=cost(MIX_FLOPS, 4 * ARRAY_BYTES),
        name="mix",
    )(received, COL, w1, b1, w2, b2, TILE, BLOCK_OF)


def back(me, here, received, slope, w1, w2):
    return pl.pallas_call(
        back_kernel,
        grid=(K8 // 2,),
        in_specs=[
            ME_SPEC,
            ME_SPEC,
            *[pl.BlockSpec(memory_space=pl.ANY)] * N,
            SLOPE_SPEC,
            full((2, H, H)),
            full((2, C, BS)),
            full((2, C, BS)),
            full((BS, C)),
            full((C, NB)),
        ],
        out_specs=[full(PIECE_SHAPE.shape)] * 8,
        out_shape=[PIECE_SHAPE] * 8,
        scratch_shapes=MIX_SCRATCH + [pltpu.VMEM((N, N, 16, C), BF), pltpu.SemaphoreType.DMA((N,))],
        cost_estimate=cost(MIX_FLOPS, 4 * ARRAY_BYTES),
        name="back",
    )(me, here, *received, slope, COL, w1, w2, TILE, BLOCK_OF)


def transposed_dot(table, value):
    return lax.dot_general(table, value, (((0,), (0,)), ((), ())), preferred_element_type=F32)


def finish_kernel(table, spec, scene, prompt, *rest):
    out = rest[-1]
    for i, j in PAIRS:
        value = transposed_dot(table[...], beside(spec[:, i].reshape(W, C), spec[:, j].reshape(W, C)))
        for row, part in ((i, value[:, :C]), (j, value[:, C:])):
            out[row] = (summed_row(scene, prompt, row).astype(F32) + part).astype(BF)


def finish(spec, scene, prompt, first, steps, into=None):
    grid_spec = pl.BlockSpec((HB, W, C), lambda i: (i + first, 0, 0))
    spec_spec = pl.BlockSpec((N, HB, 16, C), lambda i: (0, i + first, 0, 0))
    more = [] if into is None else [into]
    return pl.pallas_call(
        finish_kernel,
        grid=(steps,),
        in_specs=[full((W, W)), spec_spec, grid_spec, grid_spec] + [pl.BlockSpec(memory_space=pl.ANY)] * len(more),
        out_specs=grid_spec,
        out_shape=jax.ShapeDtypeStruct((N, W, C), BF),
        input_output_aliases={4: 0} if more else {},
        cost_estimate=cost(ROW_FLOPS * steps * HB // N, 4 * ARRAY_BYTES * steps * HB // N),
        name="finish_b" if more else "finish_a",
    )(ROW_INV, spec, scene, prompt, *more)


def grad_row_kernel(table, spec, out):
    out[...] = transposed_dot(table[...], spec[...].reshape(W, C)).astype(BF).reshape(N, 16, C)


def grad_row(spec):
    return pl.pallas_call(
        grad_row_kernel,
        grid=(1,),
        in_specs=[full((W, W)), full((N, 16, C))],
        out_specs=full((N, 16, C)),
        out_shape=jax.ShapeDtypeStruct((N, 16, C), BF),
        cost_estimate=cost(ROW_FLOPS // N, 2 * ARRAY_BYTES // N),
        name="grad_row",
    )(ROW_FWD, spec)


def along_x(j):
    return [(x * 4 + y, ((x + j) % 4) * 4 + y) for x in range(4) for y in range(4)]


def along_y(j):
    return [(x * 4 + y, x * 4 + (y + j) % 4) for x in range(4) for y in range(4)]


def shifted_sum(pieces, perm_of):
    received = [lax.ppermute(pieces[j], "dp", perm_of(j)) for j in (1, 3, 2)]
    total = pieces[0].astype(F32)
    for piece in received:
        total = total + piece.astype(F32)
    return total


def sum_over_dp(pieces):
    first = shifted_sum(pieces[:4], along_y).astype(BF)
    second = shifted_sum(pieces[4:], along_x).astype(BF)
    first = shifted_sum([first[j] for j in range(4)], along_x)
    second = shifted_sum([second[j] for j in range(4)], along_y)
    return jnp.concatenate([first, second], axis=0)


def plain_sum_over_dp(pieces):
    along = shifted_sum(pieces, along_y).astype(BF)
    return shifted_sum([along[i] for i in range(4)], along_x)


SEND_ORDER = (8, 7, 9, 6, 10, 5, 11, 4, 12, 3, 13, 2, 14, 1, 15)


def send_round(pieces):
    received = {0: pieces[0]}
    for j in SEND_ORDER:
        received[j] = lax.ppermute(pieces[j], "rows", [(i, (i + j) % N) for i in range(N)])
    return [received[j] for j in range(N)]


def exchange(blocks, axis):
    return lax.all_to_all(blocks, axis, split_axis=0, concat_axis=0, tiled=True)


def on_device(scenes, prompt, cotangent, first_weight, first_bias, second_weight, second_bias):
    scene, cot = scenes[0], cotangent[0]
    w1 = first_weight.reshape(2, C, BS)
    w2 = second_weight.reshape(2, C, BS)
    here = lax.axis_index("rows").reshape(1)
    me = lax.axis_index("dp").reshape(1)
    scene_cols = exchange(rows_scene(scene, prompt), "rows")
    leaving = rows_cot(me, here, cot)
    cot_sum = plain_sum_over_dp(leaving[N:])
    cot_cols = send_round(leaving[:N])
    scene_cols, cot_sum = lax.optimization_barrier((scene_cols, cot_sum))
    mixed_cols, slope = mix(scene_cols, w1, first_bias, w2, second_bias)
    mixed_rows = exchange(mixed_cols, "rows")
    grad_sum = sum_over_dp(back(me, here, cot_cols, slope, w1, w2)).astype(BF)
    grad_cols = exchange(grad_sum, "rows")
    mixed = finish(mixed_rows, scene, prompt, 0, FINISH_A)
    grad_rows = exchange(grad_row(grad_cols), "dp")
    mixed = finish(mixed_rows, scene, prompt, FINISH_A, N // HB - FINISH_A, mixed)
    prompt_grad = grad_rows.astype(F32) + cot_sum
    return (mixed[None], prompt_grad)


def solution(mesh):
    return jax.shard_map(
        on_device,
        mesh=mesh,
        in_specs=(
            P("dp", "rows", None, None),
            P("rows", None, None),
            P("dp", "rows", None, None),
            P(),
            P(),
            P(),
            P(),
        ),
        out_specs=(P("dp", "rows", None, None), P("rows", "dp", None)),
        check_vma=False,
    )
```

```python
import functools
import math

import jax
import jax.numpy as jnp
import numpy as np
from jax import lax
from jax.experimental import pallas as pl
from jax.experimental.pallas import tpu as pltpu
from jax.sharding import PartitionSpec as P


H = 256
W = 256
C = 384
NB = 8
BS = 48
KW = 128
N = 16
K8 = 8
BF = jnp.bfloat16
F32 = jnp.float32


def tables():
    grid = np.arange(W)
    modes = np.arange(KW)
    angles = ((modes[:, None] * grid[None, :]) % W).astype(np.float32) * np.float32(2.0 * math.pi / W)
    cosine = np.cos(angles) / np.float32(16.0)
    sine = np.sin(angles) / np.float32(16.0)
    forward = np.stack([cosine, -sine])
    doubled = np.where(modes == 0, 1.0, 2.0).astype(np.float32)[:, None]
    inverse = np.stack([doubled * cosine, -doubled * sine])

    def by_owner(table):
        return table.reshape(2, N, K8, W).transpose(1, 0, 2, 3).reshape(W, W).astype(BF)

    row_fwd, row_inv = by_owner(forward), by_owner(inverse)
    angles = ((grid[:, None] * grid[None, :]) % H).astype(np.float32) * np.float32(2.0 * math.pi / H)
    c = np.cos(angles) / np.float32(16.0)
    s = np.sin(angles) / np.float32(16.0)
    return row_fwd, row_inv, np.stack([c, s]).astype(BF)


ROW_FWD, ROW_INV, COL = tables()
TILE = (np.arange(C)[None, :] % BS == np.arange(BS)[:, None]).astype(BF)
BLOCK_OF = (np.arange(C)[:, None] // BS == np.arange(NB)[None, :]).astype(BF)


def dot(a, b):
    return jnp.dot(a, b, preferred_element_type=F32)


def cost(flops, bytes_accessed):
    return pl.CostEstimate(flops=int(flops), bytes_accessed=int(bytes_accessed), transcendentals=0)


def full(shape):
    return pl.BlockSpec(shape, lambda i: (0,) * len(shape))


HB = 4
FINISH_A = 2
PAIRS = [(i, i + 1) for i in range(0, HB, 2)]


def beside(left, right):
    return jnp.concatenate([left, right], axis=1)


def summed_row(scene, prompt, i):
    return (scene[i].astype(F32) + prompt[i].astype(F32)).astype(BF)


def put_rows(out, pair, value):
    value = value.astype(BF)
    for i, part in zip(pair, (value[:, :C], value[:, C:])):
        out[:, i] = part.reshape(N, 16, C)


def rows_scene_kernel(table, scene, prompt, out):
    for i, j in PAIRS:
        summed = beside(summed_row(scene, prompt, i), summed_row(scene, prompt, j))
        put_rows(out, (i, j), dot(table[...], summed))


def rows_cot_kernel(distances, me, here, table, cot, *rest):
    outs, pieces, ordered = rest[: len(distances)], rest[len(distances) : -1], rest[-1]

    @pl.when(pl.program_id(0) == 0)
    def _():
        for at, j in enumerate(distances):
            owner = (here[0] + j) & (N - 1)
            ordered[at * 16 : (at + 1) * 16] = table[pl.ds(pl.multiple_of(owner * 16, 16), 16), :]

    for i, j in PAIRS:
        value = dot(ordered[...], beside(cot[i], cot[j])).astype(BF)
        for at in range(len(distances)):
            part = value[at * 16 : (at + 1) * 16]
            outs[at][i] = part[:, :C]
            outs[at][j] = part[:, C:]

    x, y = me[0] >> 2, me[0] & 3

    def slot(b, carry):
        for a in range(4):
            owner = ((x + b) & 3) * 4 + ((y + a) & 3)
            rows = pl.ds(pl.multiple_of(owner * 16, 16), 16)
            for i in range(HB):
                pieces[a][b, i] = cot[i, rows, :]
        return carry

    if pieces:
        lax.fori_loop(0, 4, slot, 0)


GRID_SPEC = pl.BlockSpec((HB, W, C), lambda i: (i, 0, 0))
SPEC_SPEC = pl.BlockSpec((N, HB, 16, C), lambda i: (0, i, 0, 0))
SPEC_SHAPE = jax.ShapeDtypeStruct((N, N, 16, C), BF)
PIECE_SHAPE = jax.ShapeDtypeStruct((4, N // 2, 16, C), BF)
ROW_FLOPS = 2 * 256 * 256 * N * C
ARRAY_BYTES = 2 * N * W * C
ME_SPEC = pl.BlockSpec(memory_space=pltpu.SMEM)


def rows_scene(scene, prompt):
    return pl.pallas_call(
        rows_scene_kernel,
        grid=(N // HB,),
        in_specs=[full((W, W)), GRID_SPEC, GRID_SPEC],
        out_specs=SPEC_SPEC,
        out_shape=SPEC_SHAPE,
        cost_estimate=cost(ROW_FLOPS, 3 * ARRAY_BYTES),
        name="rows_scene",
    )(ROW_FWD, scene, prompt)


SEND_ORDER = (8, 7, 9, 6, 10, 5, 11, 4, 12, 3, 13, 2, 14, 1, 15)
EARLY = 4


def rows_cot(me, here, cot, distances, with_pieces):
    count = len(distances)
    pieces = 4 if with_pieces else 0
    return pl.pallas_call(
        functools.partial(rows_cot_kernel, distances),
        grid=(N // HB,),
        in_specs=[ME_SPEC, ME_SPEC, full((W, W)), GRID_SPEC],
        out_specs=[pl.BlockSpec((HB, 16, C), lambda i: (i, 0, 0))] * count
        + [pl.BlockSpec((4, HB, 16, C), lambda i: (0, i, 0, 0))] * pieces,
        out_shape=[jax.ShapeDtypeStruct((N, 16, C), BF)] * count
        + [jax.ShapeDtypeStruct((4, N, 16, C), BF)] * pieces,
        scratch_shapes=[pltpu.VMEM((16 * count, W), BF)],
        cost_estimate=cost(ROW_FLOPS * count // N, ARRAY_BYTES * (N + count + 4 * pieces) // N),
        name="rows_cot_late" if with_pieces else "rows_cot_early",
    )(me, here, ROW_INV, cot)


LANES = 128
TILES = C // LANES


def load_block(received, wide):
    def step(r, carry):
        rows = received[r].astype(F32).reshape(256, C)
        for t in range(TILES):
            wide[t, pl.ds(pl.multiple_of(r * 256, 256), 256), :] = rows[:, t * LANES : (t + 1) * LANES]
        return carry

    lax.fori_loop(0, N, step, 0)


def block_of(wide, r):
    rows = pl.ds(pl.multiple_of(r * 256, 256), 256)
    return jnp.concatenate([wide[t, rows, :].astype(BF) for t in range(TILES)], axis=1).reshape(N, 16, C)


def columns_of(wide, k):
    halves = []
    for q in range(2):
        parts = []
        for kk in range(2):
            rows = pl.ds(q * K8 + k + kk, H, stride=16)
            parts += [wide[t, rows, :].astype(BF) for t in range(TILES)]
        halves.append(jnp.concatenate(parts, axis=1))
    return jnp.concatenate(halves, axis=0)


def store_columns(wide, k, value):
    for q in range(2):
        for kk in range(2):
            rows = pl.ds(q * K8 + k + kk, H, stride=16)
            for t in range(TILES):
                lane = kk * C + t * LANES
                wide[t, rows, :] = value[q * H : (q + 1) * H, lane : lane + LANES]


def swap_pairs(value):
    return jnp.concatenate([beside(value[:H, :C], value[H:, :C]), beside(value[:H, C:], value[H:, C:])], axis=0)


def same_block(member):
    return lax.dot_general(member[...], member[...], (((1,), (1,)), ((), ())), preferred_element_type=F32)


def expand(weight, tile, member, dense):
    mask = same_block(member)
    real = (dot(weight[0], tile[...]) * mask).astype(BF)
    imag = (dot(weight[1], tile[...]) * mask).astype(BF)
    dense[:C, :C] = real
    dense[:C, C:] = imag
    dense[C:, :C] = -imag
    dense[C:, C:] = real


def expand_transposed(weight, tile, member, dense):
    mask = same_block(member)

    def spread(part):
        wide = lax.dot_general(tile[...], part, (((0,), (1,)), ((), ())), preferred_element_type=F32)
        return (wide * mask).astype(BF)

    real = spread(weight[0])
    imag = spread(weight[1])
    dense[:C, :C] = real
    dense[:C, C:] = -imag
    dense[C:, :C] = imag
    dense[C:, C:] = real


def mix_kernel(received, col, w1, b1, w2, b2, tile, member, out, slope, wide, dense1, dense2, col_fwd, col_inv):
    k = pl.program_id(0) * 2

    @pl.when(k == 0)
    def _():
        load_block(received, wide)
        column_matrices(col, col_fwd, col_inv)
        expand(w1, tile, member, dense1)
        expand(w2, tile, member, dense2)

    spectrum = dot(col_fwd[...], columns_of(wide, k)).astype(BF)
    bias1 = jnp.concatenate([b1[0:1], b1[1:2]], axis=1)
    bias2 = jnp.concatenate([b2[0:1], b2[1:2]], axis=1)
    z = dot(swap_pairs(spectrum), dense1[...]) + bias1
    cumulative = 0.5 * (1.0 + lax.erf(z * 0.7071067811865476))
    hidden = (z * cumulative).astype(BF)
    slope[...] = (cumulative + z * (jnp.exp(-0.5 * z * z) * 0.3989422804014327)).reshape(2, H, 2 * C)
    output = (dot(hidden, dense2[...]) + bias2).astype(BF)
    store_columns(wide, k, dot(col_inv[...], swap_pairs(output)))

    @pl.when(k == K8 - 2)
    def _():
        def step(r, carry):
            out[r] = block_of(wide, r)
            return carry

        lax.fori_loop(0, N, step, 0)


def back_kernel(me, here, *refs):
    received, (slope, col, w1, w2, tile, member), rest = refs[:N], refs[N : N + 6], refs[N + 6 :]
    pieces, (wide, dense1, dense2, col_fwd, col_inv, landed, arrived) = rest[:8], rest[8:]
    k = pl.program_id(0) * 2

    @pl.when(k == 0)
    def _():
        for j in range(N):
            pltpu.make_async_copy(received[j], landed.at[j], arrived.at[j]).start()
        column_matrices(col, col_fwd, col_inv)
        expand_transposed(w1, tile, member, dense1)
        expand_transposed(w2, tile, member, dense2)
        for j in range(N):
            pltpu.make_async_copy(received[j], landed.at[j], arrived.at[j]).wait()

        def step(j, carry):
            source = (here[0] - j) & (N - 1)
            rows = landed[j].astype(F32).reshape(256, C)
            for t in range(TILES):
                wide[t, pl.ds(pl.multiple_of(source * 256, 256), 256), :] = rows[:, t * LANES : (t + 1) * LANES]
            return carry

        lax.fori_loop(0, N, step, 0)

    back_out = dot(col_fwd[...], columns_of(wide, k)).astype(BF)
    back_pre = (dot(swap_pairs(back_out), dense2[...]) * slope[...].reshape(2 * H, 2 * C)).astype(BF)
    back_spectrum = dot(back_pre, dense1[...]).astype(BF)
    store_columns(wide, k, dot(col_inv[...], swap_pairs(back_spectrum)))

    @pl.when(k == K8 - 2)
    def _():
        x, y = me[0] >> 2, me[0] & 3
        for half in range(2):
            for a in range(4):
                for b in range(4):
                    jx, jy = (b, a) if half == 0 else (a, b)
                    owner = ((x + jx) & 3) * 4 + ((y + jy) & 3)

                    def step(r, carry, a=a, b=b, half=half, owner=owner):
                        rows = pl.ds(pl.multiple_of(((half * 8 + r) * 16 + owner) * 16, 16), 16)
                        block = jnp.concatenate([wide[t, rows, :].astype(BF) for t in range(TILES)], axis=1)
                        pieces[half * 4 + a][b, r] = block
                        return carry

                    lax.fori_loop(0, N // 2, step, 0)


def column_matrices(col, col_fwd, col_inv):
    c, s = col[0], col[1]
    for matrix, sine in ((col_fwd, s), (col_inv, -s)):
        matrix[:H, :H] = c
        matrix[:H, H:] = sine
        matrix[H:, :H] = -sine
        matrix[H:, H:] = c


MIX_FLOPS = 2 * K8 * (2 * 512 * 512 * C + 2 * 256 * 768 * 768)
MIX_SCRATCH = [
    pltpu.VMEM((TILES, H * 16, LANES), F32),
    pltpu.VMEM((2 * C, 2 * C), BF),
    pltpu.VMEM((2 * C, 2 * C), BF),
    pltpu.VMEM((2 * H, 2 * H), BF),
    pltpu.VMEM((2 * H, 2 * H), BF),
]
SLOPE_SPEC = pl.BlockSpec((2, H, 2 * C), lambda i: (i, 0, 0))
SLOPE_SHAPE = jax.ShapeDtypeStruct((K8, H, 2 * C), F32)
FULL_SPEC = full((N, N, 16, C))


def mix(received, w1, b1, w2, b2):
    return pl.pallas_call(
        mix_kernel,
        grid=(K8 // 2,),
        in_specs=[
            FULL_SPEC,
            full((2, H, H)),
            full((2, C, BS)),
            full((2, C)),
            full((2, C, BS)),
            full((2, C)),
            full((BS, C)),
            full((C, NB)),
        ],
        out_specs=[FULL_SPEC, SLOPE_SPEC],
        out_shape=[SPEC_SHAPE, SLOPE_SHAPE],
        scratch_shapes=MIX_SCRATCH,
        cost_estimate=cost(MIX_FLOPS, 4 * ARRAY_BYTES),
        name="mix",
    )(received, COL, w1, b1, w2, b2, TILE, BLOCK_OF)


def back(me, here, received, slope, w1, w2):
    return pl.pallas_call(
        back_kernel,
        grid=(K8 // 2,),
        in_specs=[
            ME_SPEC,
            ME_SPEC,
            *[pl.BlockSpec(memory_space=pl.ANY)] * N,
            SLOPE_SPEC,
            full((2, H, H)),
            full((2, C, BS)),
            full((2, C, BS)),
            full((BS, C)),
            full((C, NB)),
        ],
        out_specs=[full(PIECE_SHAPE.shape)] * 8,
        out_shape=[PIECE_SHAPE] * 8,
        scratch_shapes=MIX_SCRATCH + [pltpu.VMEM((N, N, 16, C), BF), pltpu.SemaphoreType.DMA((N,))],
        cost_estimate=cost(MIX_FLOPS, 4 * ARRAY_BYTES),
        name="back",
    )(me, here, *received, slope, COL, w1, w2, TILE, BLOCK_OF)


def transposed_dot(table, value):
    return lax.dot_general(table, value, (((0,), (0,)), ((), ())), preferred_element_type=F32)


def finish_kernel(table, spec, scene, prompt, *rest):
    out = rest[-1]
    for i, j in PAIRS:
        value = transposed_dot(table[...], beside(spec[:, i].reshape(W, C), spec[:, j].reshape(W, C)))
        for row, part in ((i, value[:, :C]), (j, value[:, C:])):
            out[row] = (summed_row(scene, prompt, row).astype(F32) + part).astype(BF)


def finish(spec, scene, prompt, first, steps, into=None):
    grid_spec = pl.BlockSpec((HB, W, C), lambda i: (i + first, 0, 0))
    spec_spec = pl.BlockSpec((N, HB, 16, C), lambda i: (0, i + first, 0, 0))
    more = [] if into is None else [into]
    return pl.pallas_call(
        finish_kernel,
        grid=(steps,),
        in_specs=[full((W, W)), spec_spec, grid_spec, grid_spec] + [pl.BlockSpec(memory_space=pl.ANY)] * len(more),
        out_specs=grid_spec,
        out_shape=jax.ShapeDtypeStruct((N, W, C), BF),
        input_output_aliases={4: 0} if more else {},
        cost_estimate=cost(ROW_FLOPS * steps * HB // N, 4 * ARRAY_BYTES * steps * HB // N),
        name="finish_b" if more else "finish_a",
    )(ROW_INV, spec, scene, prompt, *more)


def grad_row_kernel(table, spec, out):
    out[...] = transposed_dot(table[...], spec[...].reshape(W, C)).astype(BF).reshape(N, 16, C)


def grad_row(spec):
    return pl.pallas_call(
        grad_row_kernel,
        grid=(1,),
        in_specs=[full((W, W)), full((N, 16, C))],
        out_specs=full((N, 16, C)),
        out_shape=jax.ShapeDtypeStruct((N, 16, C), BF),
        cost_estimate=cost(ROW_FLOPS // N, 2 * ARRAY_BYTES // N),
        name="grad_row",
    )(ROW_FWD, spec)


def along_x(j):
    return [(x * 4 + y, ((x + j) % 4) * 4 + y) for x in range(4) for y in range(4)]


def along_y(j):
    return [(x * 4 + y, x * 4 + (y + j) % 4) for x in range(4) for y in range(4)]


def shifted_sum(pieces, perm_of):
    received = [lax.ppermute(pieces[j], "dp", perm_of(j)) for j in (1, 3, 2)]
    total = pieces[0].astype(F32)
    for piece in received:
        total = total + piece.astype(F32)
    return total


def sum_over_dp(pieces):
    first = shifted_sum(pieces[:4], along_y).astype(BF)
    second = shifted_sum(pieces[4:], along_x).astype(BF)
    first = shifted_sum([first[j] for j in range(4)], along_x)
    second = shifted_sum([second[j] for j in range(4)], along_y)
    return jnp.concatenate([first, second], axis=0)


def plain_sum_over_dp(pieces):
    along = shifted_sum(pieces, along_y).astype(BF)
    return shifted_sum([along[i] for i in range(4)], along_x)


def send_round(pieces, order):
    return {j: lax.ppermute(pieces[j], "rows", [(i, (i + j) % N) for i in range(N)]) for j in order}


def exchange(blocks, axis):
    return lax.all_to_all(blocks, axis, split_axis=0, concat_axis=0, tiled=True)


def on_device(scenes, prompt, cotangent, first_weight, first_bias, second_weight, second_bias):
    scene, cot = scenes[0], cotangent[0]
    w1 = first_weight.reshape(2, C, BS)
    w2 = second_weight.reshape(2, C, BS)
    here = lax.axis_index("rows").reshape(1)
    me = lax.axis_index("dp").reshape(1)
    early, late = SEND_ORDER[:EARLY], (0,) + SEND_ORDER[EARLY:]
    first = rows_cot(me, here, cot, early, False)
    late_scene, *first = lax.optimization_barrier((scene, *first))
    scene_cols = exchange(rows_scene(late_scene, prompt), "rows")
    last = rows_cot(me, here, cot, late, True)
    cot_sum = plain_sum_over_dp(last[len(late) :])
    last = dict(zip(late, last))
    arrived = send_round(dict(zip(early, first)), early)
    arrived |= send_round(last, late[1:]) | {0: last[0]}
    cot_cols = [arrived[j] for j in range(N)]
    scene_cols, cot_sum = lax.optimization_barrier((scene_cols, cot_sum))
    mixed_cols, slope = mix(scene_cols, w1, first_bias, w2, second_bias)
    mixed_rows = exchange(mixed_cols, "rows")
    grad_sum = sum_over_dp(back(me, here, cot_cols, slope, w1, w2)).astype(BF)
    grad_cols = exchange(grad_sum, "rows")
    mixed = finish(mixed_rows, scene, prompt, 0, FINISH_A)
    grad_rows = exchange(grad_row(grad_cols), "dp")
    mixed = finish(mixed_rows, scene, prompt, FINISH_A, N // HB - FINISH_A, mixed)
    prompt_grad = grad_rows.astype(F32) + cot_sum
    return (mixed[None], prompt_grad)


def solution(mesh):
    return jax.shard_map(
        on_device,
        mesh=mesh,
        in_specs=(
            P("dp", "rows", None, None),
            P("rows", None, None),
            P("dp", "rows", None, None),
            P(),
            P(),
            P(),
            P(),
        ),
        out_specs=(P("dp", "rows", None, None), P("rows", "dp", None)),
        check_vma=False,
    )
```
